32 devices in a mesh: lat: 4 (over z), comp: 8 (over y, x, core).
Axes of the slice: x: 2, y: 2, z: 4, core: 2. Of those that a mesh axis runs over, the one named last changes fastest.
Arguments:
- spectrum: float32 [1152, 64, 512], P('comp', 'lat'), may hold values from 0.05 to 2
- mask: int32 [64, 512], replicated, may hold values 0 or 1
- courant: float32 [2, 1152], P(None, 'comp'), may hold values from -0.5 to 0.5
- proj_a: bfloat16 [1152, 1152], P('comp'), may hold values from -0.1875 to 0.1875
- proj_b: bfloat16 [1152, 1152], P('comp'), may hold values from -0.1875 to 0.1875
- proj_c: bfloat16 [1152, 1152], P('comp'), may hold values from -0.1875 to 0.1875
- proj_d: bfloat16 [1152, 1152], P('comp'), may hold values from -0.1875 to 0.1875
- stokes_kernel: float32 [1152, 64], replicated, may hold values from -0.1875 to 0.1875
- tile_points: int32 [4, 8, 2048], P('lat', 'comp'), may hold values from 0 to 8191, as said below
- tile_counts: int32 [4, 8], P('lat', 'comp'), may hold values from 1 to 2048, as said below
- tile_nbr: int32 [4, 8, 2, 2048], P('lat', 'comp'), may hold values from 0 to 2047, as said below
- vorticity: float32 [4, 8, 64, 2048], P('lat', 'comp'), may hold values from -6 to 6
- diffusivity: float32 [4, 8, 64, 2048], P('lat', 'comp'), may hold values from 0.1 to 1
Outputs:
- spectrum_out: float32 [1152, 64, 512], P('comp', 'lat')
- ocean_force: float32 [4, 8, 64, 2048], P('lat', 'comp')
The draws below stay inside these ranges and needn't reach their ends.
Inputs may be any that keep to these rules, and one draw needn't show every extreme that they name: `mask`: 1 marks a sea cell, 0 land. `tile_points`: each entry is a point of the tile's own latitude group, numbered as in the reference program; the entries of one tile are distinct; of any block of 1024 point numbers starting at a multiple of 1024 a tile holds at most 512, and in every tile some block holds exactly 512; only the first tile_counts entries are live. `tile_counts`: in every latitude group some tile is full. `tile_nbr`: every entry is below its tile's count.
All inputs are finite; a program needn't handle non-finite values.
Results may differ from the reference program's by a relative error of at most 0.0033.
Values may be sent and summed in bfloat16 or wider, within the bound.
A program may use at most 128 MiB of HBM per device.

```python
import math
import jax
import jax.numpy as jnp
from jax import lax

K = 1152
L = 64
ADV = 2
NLON = 512
KC = 144
NR = 64
NPG = 8192
P_DEV = 1024
TILE_MOST = 2048
TILE_CAP = 512
N_LAT = 4
N_COMP = 8


def tile_layout(key):
    base = jax.random.fold_in(key, 4242)
    key_count, key_full, key_split, key_pair, key_pick, key_order, key_nbr, key_side = jax.random.split(base, 8)
    counts = jax.random.randint(key_count, (N_LAT, N_COMP), 1, TILE_MOST + 1)
    full_tile = jax.random.randint(key_full, (N_LAT,), 0, N_COMP)
    counts = jnp.where(jnp.arange(N_COMP)[None, :] == full_tile[:, None], TILE_MOST, counts).astype(jnp.int32)
    half_comp = N_COMP // 2
    first_share = jax.random.randint(key_split, (N_LAT, N_COMP, half_comp), 0, TILE_CAP + 1)
    forced_pair = jax.random.randint(key_pair, (N_LAT, N_COMP), 0, half_comp)
    forced_side = jax.random.randint(key_side, (N_LAT, N_COMP), 0, 2)
    forced_value = forced_side * TILE_CAP
    first_share = jnp.where(jnp.arange(half_comp)[None, None, :] == forced_pair[:, :, None], forced_value[:, :, None], first_share)
    shares = jnp.stack([first_share, TILE_CAP - first_share], axis=3).reshape(N_LAT, N_COMP, N_COMP)
    picks = jax.vmap(lambda single: jax.random.permutation(single, P_DEV))(jax.random.split(key_pick, N_LAT * N_COMP * N_COMP))
    picks = picks.reshape(N_LAT, N_COMP, N_COMP, P_DEV)[:, :, :, :TILE_CAP]
    owners = jnp.arange(N_COMP, dtype=jnp.int32)[None, None, :, None]
    candidates = (owners * P_DEV + picks).reshape(N_LAT, N_COMP, N_COMP * TILE_CAP)
    valid = (jnp.arange(TILE_CAP, dtype=jnp.int32)[None, None, None, :] < shares[:, :, :, None]).reshape(N_LAT, N_COMP, N_COMP * TILE_CAP)
    order = jnp.argsort(1 - valid.astype(jnp.int32), axis=2, stable=True)[:, :, :TILE_MOST]
    chosen = jnp.take_along_axis(candidates, order, axis=2)
    mixing = jax.vmap(lambda single: jax.random.permutation(single, TILE_MOST))(jax.random.split(key_order, N_LAT * N_COMP))
    mixing = mixing.reshape(N_LAT, N_COMP, TILE_MOST)
    points = jnp.take_along_axis(chosen, mixing, axis=2).astype(jnp.int32)
    shuffles = jax.vmap(lambda single: jax.random.permutation(single, TILE_MOST))(jax.random.split(key_nbr, N_LAT * N_COMP * 2))
    shuffles = shuffles.reshape(N_LAT, N_COMP, 2, TILE_MOST)
    neighbours = (shuffles % counts[:, :, None, None]).astype(jnp.int32)
    return (counts, points, neighbours)


def draw_tile_points(key, part):
    return tile_layout(key)[1]


def draw_tile_counts(key, part):
    return tile_layout(key)[0]


def draw_tile_nbr(key, part):
    return tile_layout(key)[2]


def set_ends(entries, stream_key, smallest, top_value):
    longest = entries.shape.index(max(entries.shape))
    spots = []
    for shift in (0, 1):
        where = [jax.random.randint(jax.random.fold_in(stream_key, axis), (), 0, length) for axis, length in enumerate(entries.shape)]
        where[longest] = (where[longest] + shift) % entries.shape[longest]
        spots.append(tuple(where))
    return entries.at[spots[0]].set(smallest).at[spots[1]].set(top_value)


def steps_of(own_key, dims, cuts, smallest, top_value):
    level = 1.0
    for position, blocks in cuts:
        steps = jax.random.uniform(jax.random.fold_in(jax.random.fold_in(own_key, 6), position), (blocks,), jnp.float32, smallest / len(cuts), top_value / len(cuts))
        level = level * jnp.repeat(jnp.exp(steps), dims[position] // blocks).reshape((-1,) + (1,) * (len(dims) - 1 - position))
    return level


def scatter_about(own_key, shape, width, limit, pieces=(), kind=jnp.bfloat16):
    array = width * jax.random.normal(own_key, shape, jnp.float32)
    if pieces:
        array = array * steps_of(own_key, shape, pieces, -0.22, 0.18)
    return jnp.clip(array, -limit, limit).astype(kind)


def setup_inputs(seed: int = 0) -> dict:
    splits = jax.random.split(jax.random.key(seed), 14)
    return {
        "spectrum": jnp.clip(jnp.exp(math.log(2.0) - 3.6888794 * jax.random.uniform(splits[0], (K, NR, NLON), jnp.float32) ** steps_of(splits[0], (K, NR, NLON), ((0, 8), (1, 4)), -0.2, 0.2)), 0.05, 2.0),
        "mask": set_ends((jax.random.randint(splits[1], (NR, NLON), 0, 4) < 3).astype(jnp.int32), jax.random.fold_in(splits[1], 1), 0, 1),
        "courant": jnp.clip(jax.random.uniform(splits[2], (2, K), jnp.float32, -0.5, 0.5) * steps_of(splits[2], (2, K), ((1, 8),), -0.4, 0.0), -0.5, 0.5),
        "proj_a": scatter_about(splits[3], (K, K), K ** -0.5, 0.1875, ((0, 8),)),
        "proj_b": scatter_about(splits[4], (K, K), K ** -0.5, 0.1875, ((0, 8),)),
        "proj_c": scatter_about(splits[5], (K, K), K ** -0.5, 0.1875, ((0, 8),)),
        "proj_d": scatter_about(splits[6], (K, K), K ** -0.5, 0.1875, ((0, 8),)),
        "stokes_kernel": scatter_about(splits[7], (K, L), K ** -0.5, 0.1875, (), jnp.float32),
        "tile_points": draw_tile_points(jax.random.fold_in(splits[13], 71), 0),
        "tile_counts": draw_tile_counts(jax.random.fold_in(splits[13], 71), 0),
        "tile_nbr": draw_tile_nbr(jax.random.fold_in(splits[13], 71), 0),
        "vorticity": scatter_about(splits[11], (N_LAT, N_COMP, L, TILE_MOST), 1.0, 6.0, ((0, 4), (1, 8)), jnp.float32),
        "diffusivity": jnp.clip(jnp.exp(math.log(1.0) - 2.3025851 * jax.random.uniform(splits[12], (N_LAT, N_COMP, L, TILE_MOST), jnp.float32) ** steps_of(splits[12], (N_LAT, N_COMP, L, TILE_MOST), ((0, 4), (1, 8)), -0.2, 0.2)), 0.1, 1.0),
    }


time_step = 0.25


def limiter(backward, forward):
    orient = jnp.sign(backward)
    bound = jnp.minimum(jnp.minimum(2.0 * jnp.abs(backward), orient * (backward + 2.0 * forward) / 3.0), 2.0 * orient * forward)
    return orient * jnp.maximum(bound, 0.0)


def face_flux(before, center, after, beyond, speed):
    plus_face = center + 0.5 * limiter(center - before, after - center)
    minus_face = after + 0.5 * limiter(after - beyond, center - after)
    return jnp.maximum(speed, 0.0) * plus_face + jnp.minimum(speed, 0.0) * minus_face


def lon_sweep(energy, speed, sea_part):
    flux = face_flux(jnp.roll(energy, 1, 2), energy, jnp.roll(energy, -1, 2), jnp.roll(energy, -2, 2), speed)
    return sea_part * (energy - (flux - jnp.roll(flux, 1, 2)))


def lat_sweep(padded, speed, sea_part):
    extent = padded.shape[1] - 4
    flux = face_flux(padded[:, 0:extent + 1], padded[:, 1:extent + 2], padded[:, 2:extent + 3], padded[:, 3:extent + 4], speed)
    return sea_part * (padded[:, 2:extent + 2] - (flux[:, 1:] - flux[:, :-1]))


def ocean_tile(profile, points, count, neighbours, vort_tile, diff_tile):
    slots = jnp.take(profile, points, axis=1).astype(jnp.float32)
    live = (jnp.arange(slots.shape[1], dtype=jnp.int32) < count).astype(jnp.float32)
    east = jnp.take(slots, neighbours[0], axis=1)
    north = jnp.take(slots, neighbours[1], axis=1)
    upper = jnp.concatenate([slots[:1], slots[:-1]], axis=0)
    lower = jnp.concatenate([slots[1:], jnp.zeros_like(slots[:1])], axis=0)
    return live[None, :] * (vort_tile * (east - north) + diff_tile * (upper - 2.0 * slots + lower))


def reference(spectrum, mask, courant, proj_a, proj_b, proj_c, proj_d, stokes_kernel, tile_points, tile_counts, tile_nbr, vorticity, diffusivity):
    sea_mask = mask.astype(jnp.float32)
    spectra_blocks = spectrum.reshape(N_COMP, KC, NR, NLON)
    speeds = courant.reshape(2, N_COMP, KC).transpose(1, 0, 2)

    def advect(operands):
        energy = operands[0] * sea_mask
        speed_lon = operands[1][0][:, None, None]
        speed_lat = operands[1][1][:, None, None]
        for substep in range(ADV):
            energy = lon_sweep(energy, speed_lon, sea_mask)
            padded = jnp.pad(energy, ((0, 0), (2, 2), (0, 0)))
            energy = lat_sweep(padded, speed_lat, sea_mask)
        return energy

    moved = lax.map(advect, (spectra_blocks, speeds)).reshape(K, NR, NLON)
    groups = moved.reshape(K, N_LAT, NPG).transpose(1, 0, 2)
    weight_a = proj_a.astype(jnp.float32)
    weight_b = proj_b.astype(jnp.float32)
    weight_c = proj_c.astype(jnp.float32)
    weight_d = proj_d.astype(jnp.float32)
    highest = lax.Precision.HIGHEST

    def source(band):
        first = jnp.dot(weight_a.T, band, precision=highest)
        second = jnp.dot(weight_b.T, band, precision=highest)
        product = first * second
        gain = jnp.dot(weight_c.T, product, precision=highest)
        loss = jnp.dot(weight_d.T, product, precision=highest)
        updated = band + time_step * (gain - band * loss)
        profile = jnp.dot(stokes_kernel.T, updated, precision=highest).astype(jnp.bfloat16)
        return updated, profile

    updated, profiles = lax.map(source, groups)
    spectrum_out = updated.transpose(1, 0, 2).reshape(K, NR, NLON)
    per_tile = jax.vmap(ocean_tile, in_axes=(None, 0, 0, 0, 0, 0))
    per_group = jax.vmap(per_tile, in_axes=(0, 0, 0, 0, 0, 0))
    ocean_force = per_group(profiles, tile_points, tile_counts, tile_nbr, vorticity, diffusivity)
    return spectrum_out, ocean_force
```

```python
import functools

import jax
import jax.numpy as jnp
from jax import lax
from jax.experimental import pallas as pl
from jax.experimental.pallas import tpu as pltpu
from jax.sharding import PartitionSpec as P

ADV = 2
time_step = 0.25
CB = 16
LANES = 128


def half_limited(b, f):
    t = b * (1.0 / 6.0) + f * (1.0 / 3.0)
    low = jnp.minimum(jnp.minimum(b, f), t)
    high = jnp.maximum(jnp.maximum(b, f), t)
    return jnp.maximum(low, 0.0) + jnp.minimum(high, 0.0)


def advect_kernel(rows, chunk, x_ref, up_ref, dn_ref, mask_ref, cour_ref, band_ref, e_ref, x_s):
    lon = x_ref.shape[1]
    cb = up_ref.shape[1]
    margin = 2 * ADV
    total = rows + 2 * margin
    c_lon = jnp.broadcast_to(cour_ref[:, 0:1], (cb, lon))
    c_lat = jnp.broadcast_to(cour_ref[:, 1:2], (cb, lon))
    a_lon, a_lat = jnp.abs(c_lon), jnp.abs(c_lat)
    pos_lon, pos_lat = c_lon > 0.0, c_lat > 0.0

    def lon_row(e, sea):
        nxt = pltpu.roll(e, lon - 1, 1)
        d = nxt - e
        b = jnp.where(pos_lon, pltpu.roll(d, 1, 1), pltpu.roll(d, lon - 1, 1))
        flux = c_lon * jnp.where(pos_lon, e, nxt) + a_lon * half_limited(b, d)
        return sea * (e - (flux - pltpu.roll(flux, 1, 1)))

    def sea_row(r):
        return mask_ref[pl.ds(r, 1), :]

    for j in range(lon // LANES):
        x_s[j] = x_ref[:, j * LANES : (j + 1) * LANES]

    for r in range(margin):
        sea = sea_row(r)
        e_ref[r] = lon_row(up_ref[r].astype(jnp.float32) * sea, sea)
        sea = sea_row(margin + rows + r)
        e_ref[margin + rows + r] = lon_row(dn_ref[r].astype(jnp.float32) * sea, sea)

    @pl.loop(0, rows)
    def _(r):
        sea = sea_row(margin + r)
        own = jnp.concatenate([x_s[j, pl.ds(r, cb, stride=rows), :] for j in range(lon // LANES)], axis=1)
        e_ref[margin + r] = lon_row(own * sea, sea)

    def face(e0, e1, dm, d, dp):
        b = jnp.where(pos_lat, dm, dp)
        return c_lat * jnp.where(pos_lat, e0, e1) + a_lat * half_limited(b, d)

    def lat_sweep(first, last, finish):
        em, e0, e1 = e_ref[first - 2], e_ref[first - 1], e_ref[first]
        e2 = e_ref[first + 1]
        d0 = e1 - e0
        d1 = e2 - e1
        flux = face(e0, e1, e0 - em, d0, d1)

        def step(r, carry):
            cur, nxt, dm, d, before = carry
            beyond = e_ref[r + 2]
            dp = beyond - nxt
            flux = face(cur, nxt, dm, d, dp)
            finish(r, cur - (flux - before), sea_row(r))
            return nxt, beyond, d, dp, flux

        lax.fori_loop(first, last, step, (e1, e2, d0, d1, flux))

    for substep in range(ADV):
        gone = 2 * (substep + 1)
        last_one = substep == ADV - 1

        def finish(r, value, sea):
            value = sea * value
            if not last_one:
                value = lon_row(value, sea)
            e_ref[r] = value

        lat_sweep(gone, total - gone, finish)
    dests = band_ref.shape[0]
    for d in range(dests):
        at = 0
        while at < chunk:
            point = d * chunk + at
            r, lane = point // lon, point % lon
            n = min(lon - lane, chunk - at)
            v = e_ref[margin + r][:, lane : lane + n]
            band_ref[d, :, at : at + n] = v
            at += n


def advect(spectrum, halo_up, halo_dn, mask_rows, cour, dests):
    comps, rows, lon = spectrum.shape
    chunk = rows * lon // dests
    margin = 2 * ADV
    total = rows + 2 * margin
    blk = pl.BlockSpec((dests, CB, chunk), lambda i: (0, i, 0))
    return pl.pallas_call(
        functools.partial(advect_kernel, rows, chunk),
        grid=(pl.cdiv(comps, CB),),
        in_specs=[
            pl.BlockSpec((CB * rows, lon), lambda i: (i, 0)),
            pl.BlockSpec((margin, CB, lon), lambda i: (0, i, 0)),
            pl.BlockSpec((margin, CB, lon), lambda i: (0, i, 0)),
            pl.BlockSpec((total, lon), lambda i: (0, 0)),
            pl.BlockSpec((CB, 2), lambda i: (i, 0)),
        ],
        out_specs=blk,
        out_shape=jax.ShapeDtypeStruct((dests, comps, chunk), jnp.float32),
        scratch_shapes=[
            pltpu.VMEM((total, CB, lon), jnp.float32),
            pltpu.VMEM((lon // LANES, CB * rows, LANES), jnp.float32),
        ],
        name="advect",
    )(spectrum.reshape(comps * rows, lon), halo_up, halo_dn, mask_rows, cour)


def finish_kernel(rows, band_ref, delta_ref, out_ref, o_s):
    dests, cb, chunk = band_ref.shape
    lon = out_ref.shape[1]
    for d in range(dests):
        at = 0
        while at < chunk:
            point = d * chunk + at
            r, lane = point // lon, point % lon
            n = min(lon - lane, chunk - at)
            v = band_ref[d, :, at : at + n] + delta_ref[d, :, at : at + n].astype(jnp.float32)
            for j in range(n // LANES):
                o_s[lane // LANES + j, pl.ds(r, cb, stride=rows), :] = v[:, j * LANES : (j + 1) * LANES]
            at += n
    for j in range(lon // LANES):
        out_ref[:, j * LANES : (j + 1) * LANES] = o_s[j]


def finish(band, delta, rows, lon):
    dests, comps, chunk = band.shape
    blk = pl.BlockSpec((dests, CB, chunk), lambda i: (0, i, 0))
    out = pl.pallas_call(
        functools.partial(finish_kernel, rows),
        grid=(pl.cdiv(comps, CB),),
        in_specs=[blk, blk],
        out_specs=pl.BlockSpec((CB * rows, lon), lambda i: (i, 0)),
        out_shape=jax.ShapeDtypeStruct((comps * rows, lon), jnp.float32),
        scratch_shapes=[pltpu.VMEM((lon // LANES, CB * rows, LANES), jnp.float32)],
        name="finish",
    )(band, delta)
    return out.reshape(comps, rows, lon)


NT = (((1,), (1,)), ((), ()))


def slots_kernel(prof_ref, pts_ref, out_ref):
    jb = pts_ref.shape[0]
    layers, points = prof_ref.shape
    step = min(512, points)
    pts = jnp.broadcast_to(pts_ref[...], (jb, step))
    lane = lax.broadcasted_iota(jnp.int32, (jb, step), 1)

    def body(k, acc):
        hot = jnp.where(pts - k * step == lane, 1.0, 0.0).astype(jnp.bfloat16)
        return acc + lax.dot_general(
            hot, prof_ref[:, pl.ds(pl.multiple_of(k * step, step), step)], NT, preferred_element_type=jnp.float32
        )

    acc = lax.fori_loop(0, points // step, body, jnp.zeros((jb, layers), jnp.float32))
    out_ref[...] = acc.astype(jnp.bfloat16)


def tile_kernel(all_ref, own_ref, east_ref, north_ref, live_ref, vort_ref, diff_ref, out_ref):
    jb = own_ref.shape[0]
    slots, layers = all_ref.shape
    step = min(512, slots)
    east = jnp.broadcast_to(east_ref[...], (jb, step))
    north = jnp.broadcast_to(north_ref[...], (jb, step))
    lane = lax.broadcasted_iota(jnp.int32, (jb, step), 1)

    def body(k, acc):
        one = jnp.where(east - k * step == lane, 1.0, 0.0)
        two = jnp.where(north - k * step == lane, 1.0, 0.0)
        rows = all_ref[pl.ds(pl.multiple_of(k * step, step), step), :]
        return acc + lax.dot_general(
            (one - two).astype(jnp.bfloat16), rows, (((1,), (0,)), ((), ())), preferred_element_type=jnp.float32
        )

    acc = lax.fori_loop(0, slots // step, body, jnp.zeros((jb, layers), jnp.float32))
    gap = acc.T
    s = own_ref[...].astype(jnp.float32).T
    upper = jnp.concatenate([s[:1], s[:-1]], axis=0)
    lower = jnp.concatenate([s[1:], jnp.zeros_like(s[:1])], axis=0)
    out_ref[...] = live_ref[...] * (vort_ref[...] * gap + diff_ref[...] * (upper - 2.0 * s + lower))


def ocean(profile, pts, count, nbr, vort, diff):
    layers, points = profile.shape
    slots = pts.shape[0]
    jb = min(256, slots)
    grid = (slots // jb,)
    picked = pl.pallas_call(
        slots_kernel,
        grid=grid,
        in_specs=[
            pl.BlockSpec((layers, points), lambda j: (0, 0)),
            pl.BlockSpec((jb, 1), lambda j: (j, 0)),
        ],
        out_specs=pl.BlockSpec((jb, layers), lambda j: (j, 0)),
        out_shape=jax.ShapeDtypeStruct((slots, layers), jnp.bfloat16),
        name="slots",
    )(profile, pts[:, None])
    live = (jnp.arange(slots, dtype=jnp.int32) < count).astype(jnp.float32)[None]
    col = pl.BlockSpec((jb, 1), lambda j: (j, 0))
    wide = pl.BlockSpec((layers, jb), lambda j: (0, j))
    return pl.pallas_call(
        tile_kernel,
        grid=grid,
        in_specs=[
            pl.BlockSpec((slots, layers), lambda j: (0, 0)),
            pl.BlockSpec((jb, layers), lambda j: (j, 0)),
            col,
            col,
            pl.BlockSpec((1, jb), lambda j: (0, j)),
            wide,
            wide,
        ],
        out_specs=wide,
        out_shape=jax.ShapeDtypeStruct((layers, slots), jnp.float32),
        name="tile",
    )(picked, picked, nbr[0][:, None], nbr[1][:, None], live, vort, diff)


def contract(weights, operand):
    return lax.dot_general(
        weights, operand, (((0,), (0,)), ((), ())), preferred_element_type=jnp.float32
    )


def on_device(
    spectrum,
    mask,
    courant,
    proj_a,
    proj_b,
    proj_c,
    proj_d,
    stokes_kernel,
    tile_points,
    tile_counts,
    tile_nbr,
    vorticity,
    diffusivity,
):
    comps, rows, lon = spectrum.shape
    margin = 2 * ADV
    bands, dests = lax.axis_size("lat"), lax.axis_size("comp")
    band_index = lax.axis_index("lat")
    sea = jnp.pad(mask.astype(jnp.float32), ((margin, margin), (0, 0)))
    mask_rows = lax.dynamic_slice_in_dim(sea, band_index * rows, rows + 2 * margin, 0)
    up = [(i, i + 1) for i in range(bands - 1)]
    down = [(j, i) for i, j in up]

    def edge(part):
        return part.astype(jnp.bfloat16).transpose(1, 0, 2)

    halo_up = lax.ppermute(edge(spectrum[:, rows - margin :]), "lat", up)
    halo_dn = lax.ppermute(edge(spectrum[:, :margin]), "lat", down)
    weights = [lax.all_gather(w, "comp", axis=0, tiled=True) for w in (proj_a, proj_b, proj_c, proj_d)]
    band = advect(spectrum, halo_up, halo_dn, mask_rows, courant.T, dests)
    points = lax.all_to_all(band.astype(jnp.float16), "comp", split_axis=0, concat_axis=0)
    chunk = points.shape[2]
    points = points.reshape(dests * comps, chunk)
    own = points.astype(jnp.float32)
    points = own.astype(jnp.bfloat16)
    product = (contract(weights[0], points) * contract(weights[1], points)).astype(jnp.bfloat16)
    delta = time_step * (contract(weights[2], product) - own * contract(weights[3], product))
    profile = lax.dot_general(
        stokes_kernel, own + delta, (((0,), (0,)), ((), ())), precision=lax.Precision.HIGHEST
    ).astype(jnp.bfloat16)
    group = lax.all_gather(profile, "comp", axis=1, tiled=True)
    back = lax.all_to_all(
        delta.astype(jnp.bfloat16).reshape(dests, comps, chunk), "comp", split_axis=0, concat_axis=0
    )
    force = ocean(group, tile_points[0, 0], tile_counts[0, 0], tile_nbr[0, 0], vorticity[0, 0], diffusivity[0, 0])
    return finish(band, back, rows, lon), force[None, None]


def solution(mesh):
    return jax.shard_map(
        on_device,
        mesh=mesh,
        in_specs=(
            P("comp", "lat", None),
            P(),
            P(None, "comp"),
            P("comp", None),
            P("comp", None),
            P("comp", None),
            P("comp", None),
            P(),
            P("lat", "comp", None),
            P("lat", "comp"),
            P("lat", "comp", None, None),
            P("lat", "comp", None, None),
            P("lat", "comp", None, None),
        ),
        out_specs=(P("comp", "lat", None), P("lat", "comp", None, None)),
        check_vma=False,
    )
```

```python
import functools

import jax
import jax.numpy as jnp
from jax import lax
from jax.experimental import pallas as pl
from jax.experimental.pallas import tpu as pltpu
from jax.sharding import PartitionSpec as P

ADV = 2
time_step = 0.25
CB = 16
LANES = 128
LOW = 256


def half_limited(b, f):
    t = b * (1.0 / 6.0) + f * (1.0 / 3.0)
    low = jnp.minimum(jnp.minimum(b, f), t)
    high = jnp.maximum(jnp.maximum(b, f), t)
    return jnp.maximum(low, 0.0) + jnp.minimum(high, 0.0)


def advect_kernel(rows, chunk, x_ref, up_ref, dn_ref, mask_ref, cour_ref, band_ref, a_s, b_s, u_s, x_s):
    lon = x_ref.shape[1]
    margin = 2 * ADV
    total = rows + 2 * margin
    dests = band_ref.shape[0]
    for j in range(lon // LANES):
        x_s[j] = x_ref[:, j * LANES : (j + 1) * LANES]
    for r in range(margin):
        u_s[r] = up_ref[r].astype(jnp.float32)
        u_s[margin + r] = dn_ref[r].astype(jnp.float32)

    def wide(column):
        return jnp.concatenate([jnp.broadcast_to(column, (8, LANES))] * (lon // LANES), axis=1)

    @pl.loop(0, CB // 8)
    def _(half):
        base = pl.multiple_of(half * 8, 8)
        cour = cour_ref[pl.ds(base, 8), :]
        c_lon, c_lat = wide(cour[:, 0:1]), wide(cour[:, 1:2])
        a_lon, a_lat = jnp.abs(c_lon), jnp.abs(c_lat)
        pos_lon, pos_lat = c_lon > 0.0, c_lat > 0.0

        def sea_row(r):
            return mask_ref[r : r + 1, :]

        def lon_row(e, sea):
            nxt = pltpu.roll(e, lon - 1, 1)
            d = nxt - e
            b = jnp.where(pos_lon, pltpu.roll(d, 1, 1), pltpu.roll(d, lon - 1, 1))
            flux = c_lon * jnp.where(pos_lon, e, nxt) + a_lon * half_limited(b, d)
            return sea * (e - (flux - pltpu.roll(flux, 1, 1)))

        def start_row(r):
            if r < margin:
                return u_s[r, pl.ds(base, 8), :]
            if r >= margin + rows:
                return u_s[r - rows, pl.ds(base, 8), :]
            first = half * (8 * rows) + (r - margin)
            return jnp.concatenate(
                [x_s[j, pl.ds(first, 8, stride=rows), :] for j in range(lon // LANES)], axis=1
            )

        def store_row(r, value):
            at = 0
            while at < lon:
                d, lane = divmod((r - margin) * lon + at, chunk)
                n = min(chunk - lane, lon - at)
                band_ref[d, pl.ds(base, 8), lane : lane + n] = value[:, at : at + n]
                at += n

        for substep in range(ADV):
            gone = 2 * substep
            for r in range(gone, total - gone):
                sea = sea_row(r)
                e = start_row(r) * sea if substep == 0 else b_s[r]
                a_s[r] = lon_row(e, sea)
            cur, nxt = a_s[gone], a_s[gone + 1]
            d = nxt - cur
            dm, before = d, None
            for r in range(gone + 1, total - gone - 2):
                cur, nxt, dm = nxt, a_s[r + 1], d
                d = nxt - cur
                dp = a_s[r + 2] - nxt
                b = jnp.where(pos_lat, dm, dp)
                flux = c_lat * jnp.where(pos_lat, cur, nxt) + a_lat * half_limited(b, d)
                if before is not None:
                    value = sea_row(r) * (cur - (flux - before))
                    if substep == ADV - 1:
                        store_row(r, value)
                    else:
                        b_s[r] = value
                before = flux


def advect(spectrum, halo_up, halo_dn, mask_rows, cour, dests):
    comps, rows, lon = spectrum.shape
    chunk = rows * lon // dests
    margin = 2 * ADV
    total = rows + 2 * margin
    blk = pl.BlockSpec((dests, CB, chunk), lambda i: (0, i, 0))
    return pl.pallas_call(
        functools.partial(advect_kernel, rows, chunk),
        grid=(pl.cdiv(comps, CB),),
        in_specs=[
            pl.BlockSpec((CB * rows, lon), lambda i: (i, 0)),
            pl.BlockSpec((margin, CB, lon), lambda i: (0, i, 0)),
            pl.BlockSpec((margin, CB, lon), lambda i: (0, i, 0)),
            pl.BlockSpec((total, lon), lambda i: (0, 0)),
            pl.BlockSpec((CB, 2), lambda i: (i, 0)),
        ],
        out_specs=blk,
        out_shape=jax.ShapeDtypeStruct((dests, comps, chunk), jnp.float32),
        scratch_shapes=[
            pltpu.VMEM((total, 8, lon), jnp.float32),
            pltpu.VMEM((total, 8, lon), jnp.float32),
            pltpu.VMEM((2 * margin, CB, lon), jnp.float32),
            pltpu.VMEM((lon // LANES, CB * rows, LANES), jnp.float32),
        ],
        name="advect",
    )(spectrum.reshape(comps * rows, lon), halo_up, halo_dn, mask_rows, cour)


def finish_kernel(rows, band_ref, delta_ref, out_ref, o_s):
    dests, cb, chunk = band_ref.shape
    lon = out_ref.shape[1]
    for d in range(dests):
        at = 0
        while at < chunk:
            point = d * chunk + at
            r, lane = point // lon, point % lon
            n = min(lon - lane, chunk - at)
            v = band_ref[d, :, at : at + n] + delta_ref[d, :, at : at + n].astype(jnp.float32)
            for j in range(n // LANES):
                o_s[lane // LANES + j, pl.ds(r, cb, stride=rows), :] = v[:, j * LANES : (j + 1) * LANES]
            at += n
    for j in range(lon // LANES):
        out_ref[:, j * LANES : (j + 1) * LANES] = o_s[j]


def finish(band, delta, rows, lon):
    dests, comps, chunk = band.shape
    blk = pl.BlockSpec((dests, CB, chunk), lambda i: (0, i, 0))
    out = pl.pallas_call(
        functools.partial(finish_kernel, rows),
        grid=(pl.cdiv(comps, CB),),
        in_specs=[blk, blk],
        out_specs=pl.BlockSpec((CB * rows, lon), lambda i: (i, 0)),
        out_shape=jax.ShapeDtypeStruct((comps * rows, lon), jnp.float32),
        scratch_shapes=[pltpu.VMEM((lon // LANES, CB * rows, LANES), jnp.float32)],
        name="finish",
    )(band, delta)
    return out.reshape(comps, rows, lon)


NT = (((1,), (1,)), ((), ()))


def ocean_kernel(prof_ref, pts_ref, east_ref, north_ref, live_ref, vort_ref, diff_ref, out_ref, p_s, s_s):
    layers, points = prof_ref.shape
    slots = pts_ref.shape[0]
    per = LOW // layers
    for k in range(points // LOW):
        p_s[k * layers : (k + 1) * layers, :] = prof_ref[:, k * LOW : (k + 1) * LOW]
    lane = lax.broadcasted_iota(jnp.int32, (LOW, LOW), 1)
    block = lane // layers

    def pick(index, count, product):
        low = jnp.broadcast_to(index % LOW, (LOW, LOW))
        high = jnp.broadcast_to(index // LOW, (LOW, LOW)) - block
        hot = jnp.where(low == lane, 1.0, 0.0).astype(jnp.bfloat16)
        acc = jnp.zeros((LOW, LOW), jnp.float32)
        for m in range(-(-count // per)):
            acc = acc + jnp.where(high == m * per, product(hot, m), 0.0)
        return sum(acc[:, i * layers : (i + 1) * layers] for i in range(per))

    def from_points(hot, m):
        return lax.dot_general(hot, p_s[m * LOW : (m + 1) * LOW, :], NT, preferred_element_type=jnp.float32)

    s_s[...] = jnp.zeros_like(s_s)
    for j in range(slots // LOW):
        s = pick(pts_ref[j * LOW : (j + 1) * LOW, :], points // LOW, from_points)
        s_s[:, j * layers : (j + 1) * layers] = s.astype(jnp.bfloat16)

    def from_slots(hot, m):
        return jnp.dot(hot, s_s[:, m * LOW : (m + 1) * LOW], preferred_element_type=jnp.float32)

    for j in range(slots // LOW):
        rows = slice(j * LOW, (j + 1) * LOW)
        gap = pick(east_ref[rows, :], slots // LOW, from_slots) - pick(north_ref[rows, :], slots // LOW, from_slots)
        gap = gap.T
        s = s_s[:, j * layers : (j + 1) * layers].astype(jnp.float32).T
        upper = jnp.concatenate([s[:1], s[:-1]], axis=0)
        lower = jnp.concatenate([s[1:], jnp.zeros_like(s[:1])], axis=0)
        out_ref[:, rows] = live_ref[:, rows] * (
            vort_ref[:, rows] * gap + diff_ref[:, rows] * (upper - 2.0 * s + lower)
        )


def ocean(profile, pts, count, nbr, vort, diff):
    layers, points = profile.shape
    slots = pts.shape[0]
    per = LOW // layers
    lanes = -(-(slots // LOW) // per) * LOW
    live = (jnp.arange(slots, dtype=jnp.int32) < count).astype(jnp.float32)[None]
    return pl.pallas_call(
        ocean_kernel,
        out_shape=jax.ShapeDtypeStruct((layers, slots), jnp.float32),
        scratch_shapes=[
            pltpu.VMEM((points // LOW * layers, LOW), jnp.bfloat16),
            pltpu.VMEM((LOW, lanes), jnp.bfloat16),
        ],
        name="ocean",
    )(profile, pts[:, None], nbr[0][:, None], nbr[1][:, None], live, vort, diff)


def contract(weights, operand):
    return lax.dot_general(
        weights, operand, (((0,), (0,)), ((), ())), preferred_element_type=jnp.float32
    )


def on_device(
    spectrum,
    mask,
    courant,
    proj_a,
    proj_b,
    proj_c,
    proj_d,
    stokes_kernel,
    tile_points,
    tile_counts,
    tile_nbr,
    vorticity,
    diffusivity,
):
    comps, rows, lon = spectrum.shape
    margin = 2 * ADV
    bands, dests = lax.axis_size("lat"), lax.axis_size("comp")
    band_index = lax.axis_index("lat")
    sea = jnp.pad(mask.astype(jnp.float32), ((margin, margin), (0, 0)))
    mask_rows = lax.dynamic_slice_in_dim(sea, band_index * rows, rows + 2 * margin, 0)
    up = [(i, i + 1) for i in range(bands - 1)]
    down = [(j, i) for i, j in up]

    def edge(part):
        return lax.optimization_barrier(part).astype(jnp.bfloat16).transpose(1, 0, 2)

    halo_up = lax.ppermute(edge(spectrum[:, rows - margin :]), "lat", up)
    halo_dn = lax.ppermute(edge(spectrum[:, :margin]), "lat", down)
    weights = [lax.all_gather(w, "comp", axis=0, tiled=True) for w in (proj_a, proj_b, proj_c, proj_d)]
    band = advect(spectrum, halo_up, halo_dn, mask_rows, courant.T, dests)
    points = lax.all_to_all(band.astype(jnp.float16), "comp", split_axis=0, concat_axis=0)
    chunk = points.shape[2]
    points = points.reshape(dests * comps, chunk)
    own = points.astype(jnp.float32)
    points = own.astype(jnp.bfloat16)
    product = (contract(weights[0], points) * contract(weights[1], points)).astype(jnp.bfloat16)
    delta = time_step * (contract(weights[2], product) - own * contract(weights[3], product))
    profile = lax.dot_general(
        stokes_kernel, own + delta, (((0,), (0,)), ((), ())), precision=lax.Precision.HIGHEST
    ).astype(jnp.bfloat16)
    group = lax.all_gather(profile, "comp", axis=1, tiled=True)
    back = lax.all_to_all(
        delta.astype(jnp.bfloat16).reshape(dests, comps, chunk), "comp", split_axis=0, concat_axis=0
    )
    force = ocean(group, tile_points[0, 0], tile_counts[0, 0], tile_nbr[0, 0], vorticity[0, 0], diffusivity[0, 0])
    return finish(band, back, rows, lon), force[None, None]


def solution(mesh):
    return jax.shard_map(
        on_device,
        mesh=mesh,
        in_specs=(
            P("comp", "lat", None),
            P(),
            P(None, "comp"),
            P("comp", None),
            P("comp", None),
            P("comp", None),
            P("comp", None),
            P(),
            P("lat", "comp", None),
            P("lat", "comp"),
            P("lat", "comp", None, None),
            P("lat", "comp", None, None),
            P("lat", "comp", None, None),
        ),
        out_specs=(P("comp", "lat", None), P("lat", "comp", None, None)),
        check_vma=False,
    )
```

```python
import functools

import jax
import jax.numpy as jnp
from jax import lax
from jax.experimental import pallas as pl
from jax.experimental.pallas import tpu as pltpu
from jax.sharding import PartitionSpec as P

ADV = 2
time_step = 0.25
CB = 16
LANES = 128
LOW = 256
PIECES = 2


def half_limited(b, f):
    t = b * (1.0 / 6.0) + f * (1.0 / 3.0)
    low = jnp.minimum(jnp.minimum(b, f), t)
    high = jnp.maximum(jnp.maximum(b, f), t)
    return jnp.maximum(low, 0.0) + jnp.minimum(high, 0.0)


def advect_kernel(rows, chunk, x_ref, up_ref, dn_ref, mask_ref, cour_ref, band_ref, a_s, b_s, u_s, x_s):
    lon = x_ref.shape[1]
    margin = 2 * ADV
    total = rows + 2 * margin
    dests = band_ref.shape[0]
    for j in range(lon // LANES):
        x_s[j] = x_ref[:, j * LANES : (j + 1) * LANES]
    for r in range(margin):
        u_s[r] = up_ref[r].astype(jnp.float32)
        u_s[margin + r] = dn_ref[r].astype(jnp.float32)

    def wide(column):
        return jnp.concatenate([jnp.broadcast_to(column, (8, LANES))] * (lon // LANES), axis=1)

    @pl.loop(0, CB // 8)
    def _(half):
        base = pl.multiple_of(half * 8, 8)
        cour = cour_ref[pl.ds(base, 8), :]
        c_lon, c_lat = wide(cour[:, 0:1]), wide(cour[:, 1:2])
        a_lon, a_lat = jnp.abs(c_lon), jnp.abs(c_lat)
        pos_lon, pos_lat = c_lon > 0.0, c_lat > 0.0

        def sea_row(r):
            return mask_ref[r : r + 1, :]

        def lon_row(e, sea):
            nxt = pltpu.roll(e, lon - 1, 1)
            d = nxt - e
            b = jnp.where(pos_lon, pltpu.roll(d, 1, 1), pltpu.roll(d, lon - 1, 1))
            flux = c_lon * jnp.where(pos_lon, e, nxt) + a_lon * half_limited(b, d)
            return sea * (e - (flux - pltpu.roll(flux, 1, 1)))

        def start_row(r):
            if r < margin:
                return u_s[r, pl.ds(base, 8), :]
            if r >= margin + rows:
                return u_s[r - rows, pl.ds(base, 8), :]
            first = half * (8 * rows) + (r - margin)
            return jnp.concatenate(
                [x_s[j, pl.ds(first, 8, stride=rows), :] for j in range(lon // LANES)], axis=1
            )

        def store_row(r, value):
            at = 0
            while at < lon:
                d, lane = divmod((r - margin) * lon + at, chunk)
                n = min(chunk - lane, lon - at)
                band_ref[d, pl.ds(base, 8), lane : lane + n] = value[:, at : at + n]
                at += n

        for substep in range(ADV):
            gone = 2 * substep
            for r in range(gone, total - gone):
                sea = sea_row(r)
                e = start_row(r) * sea if substep == 0 else b_s[r]
                a_s[r] = lon_row(e, sea)
            cur, nxt = a_s[gone], a_s[gone + 1]
            d = nxt - cur
            dm, before = d, None
            for r in range(gone + 1, total - gone - 2):
                cur, nxt, dm = nxt, a_s[r + 1], d
                d = nxt - cur
                dp = a_s[r + 2] - nxt
                b = jnp.where(pos_lat, dm, dp)
                flux = c_lat * jnp.where(pos_lat, cur, nxt) + a_lat * half_limited(b, d)
                if before is not None:
                    value = sea_row(r) * (cur - (flux - before))
                    if substep == ADV - 1:
                        store_row(r, value)
                    else:
                        b_s[r] = value
                before = flux


def advect(spectrum, halo_up, halo_dn, mask_rows, cour, dests, first, size):
    comps, rows, lon = spectrum.shape
    chunk = rows * lon // dests
    margin = 2 * ADV
    skip = first // CB
    total = rows + 2 * margin
    blk = pl.BlockSpec((dests, CB, chunk), lambda i: (0, i, 0))
    return pl.pallas_call(
        functools.partial(advect_kernel, rows, chunk),
        grid=(pl.cdiv(size, CB),),
        in_specs=[
            pl.BlockSpec((CB * rows, lon), lambda i: (i + skip, 0)),
            pl.BlockSpec((margin, CB, lon), lambda i: (0, i + skip, 0)),
            pl.BlockSpec((margin, CB, lon), lambda i: (0, i + skip, 0)),
            pl.BlockSpec((total, lon), lambda i: (0, 0)),
            pl.BlockSpec((CB, 2), lambda i: (i + skip, 0)),
        ],
        out_specs=blk,
        out_shape=jax.ShapeDtypeStruct((dests, size, chunk), jnp.float32),
        scratch_shapes=[
            pltpu.VMEM((total, 8, lon), jnp.float32),
            pltpu.VMEM((total, 8, lon), jnp.float32),
            pltpu.VMEM((2 * margin, CB, lon), jnp.float32),
            pltpu.VMEM((lon // LANES, CB * rows, LANES), jnp.float32),
        ],
        cost_estimate=pl.CostEstimate(
            flops=size * rows * lon * 400, bytes_accessed=size * rows * lon * 8, transcendentals=0
        ),
        name="advect",
    )(spectrum.reshape(comps * rows, lon), halo_up, halo_dn, mask_rows, cour)


def finish_kernel(rows, band_ref, delta_ref, out_ref, o_s):
    dests, cb, chunk = band_ref.shape
    lon = out_ref.shape[1]
    for d in range(dests):
        at = 0
        while at < chunk:
            point = d * chunk + at
            r, lane = point // lon, point % lon
            n = min(lon - lane, chunk - at)
            v = band_ref[d, :, at : at + n] + delta_ref[d, :, at : at + n].astype(jnp.float32)
            for j in range(n // LANES):
                o_s[lane // LANES + j, pl.ds(r, cb, stride=rows), :] = v[:, j * LANES : (j + 1) * LANES]
            at += n
    for j in range(lon // LANES):
        out_ref[:, j * LANES : (j + 1) * LANES] = o_s[j]


def finish(band, delta, rows, lon):
    dests, comps, chunk = band.shape
    blk = pl.BlockSpec((dests, CB, chunk), lambda i: (0, i, 0))
    out = pl.pallas_call(
        functools.partial(finish_kernel, rows),
        grid=(pl.cdiv(comps, CB),),
        in_specs=[blk, blk],
        out_specs=pl.BlockSpec((CB * rows, lon), lambda i: (i, 0)),
        out_shape=jax.ShapeDtypeStruct((comps * rows, lon), jnp.float32),
        scratch_shapes=[pltpu.VMEM((lon // LANES, CB * rows, LANES), jnp.float32)],
        name="finish",
    )(band, delta)
    return out.reshape(comps, rows, lon)


NT = (((1,), (1,)), ((), ()))


def ocean_kernel(prof_ref, pts_ref, east_ref, north_ref, live_ref, vort_ref, diff_ref, out_ref, p_s, s_s):
    layers, points = prof_ref.shape
    slots = pts_ref.shape[0]
    per = LOW // layers
    for k in range(points // LOW):
        p_s[k * layers : (k + 1) * layers, :] = prof_ref[:, k * LOW : (k + 1) * LOW]
    lane = lax.broadcasted_iota(jnp.int32, (LOW, LOW), 1)
    block = lane // layers

    def pick(index, count, product):
        low = jnp.broadcast_to(index % LOW, (LOW, LOW))
        high = jnp.broadcast_to(index // LOW, (LOW, LOW)) - block
        hot = jnp.where(low == lane, 1.0, 0.0).astype(jnp.bfloat16)
        acc = jnp.zeros((LOW, LOW), jnp.float32)
        for m in range(-(-count // per)):
            acc = acc + jnp.where(high == m * per, product(hot, m), 0.0)
        return sum(acc[:, i * layers : (i + 1) * layers] for i in range(per))

    def from_points(hot, m):
        return lax.dot_general(hot, p_s[m * LOW : (m + 1) * LOW, :], NT, preferred_element_type=jnp.float32)

    s_s[...] = jnp.zeros_like(s_s)
    for j in range(slots // LOW):
        s = pick(pts_ref[j * LOW : (j + 1) * LOW, :], points // LOW, from_points)
        s_s[:, j * layers : (j + 1) * layers] = s.astype(jnp.bfloat16)

    def from_slots(hot, m):
        return jnp.dot(hot, s_s[:, m * LOW : (m + 1) * LOW], preferred_element_type=jnp.float32)

    for j in range(slots // LOW):
        rows = slice(j * LOW, (j + 1) * LOW)
        gap = pick(east_ref[rows, :], slots // LOW, from_slots) - pick(north_ref[rows, :], slots // LOW, from_slots)
        gap = gap.T
        s = s_s[:, j * layers : (j + 1) * layers].astype(jnp.float32).T
        upper = jnp.concatenate([s[:1], s[:-1]], axis=0)
        lower = jnp.concatenate([s[1:], jnp.zeros_like(s[:1])], axis=0)
        out_ref[:, rows] = live_ref[:, rows] * (
            vort_ref[:, rows] * gap + diff_ref[:, rows] * (upper - 2.0 * s + lower)
        )


def ocean(profile, pts, count, nbr, vort, diff):
    layers, points = profile.shape
    slots = pts.shape[0]
    per = LOW // layers
    lanes = -(-(slots // LOW) // per) * LOW
    live = (jnp.arange(slots, dtype=jnp.int32) < count).astype(jnp.float32)[None]
    return pl.pallas_call(
        ocean_kernel,
        out_shape=jax.ShapeDtypeStruct((layers, slots), jnp.float32),
        scratch_shapes=[
            pltpu.VMEM((points // LOW * layers, LOW), jnp.bfloat16),
            pltpu.VMEM((LOW, lanes), jnp.bfloat16),
        ],
        name="ocean",
    )(profile, pts[:, None], nbr[0][:, None], nbr[1][:, None], live, vort, diff)


def contract(weights, operand):
    return lax.dot_general(
        weights, operand, (((0,), (0,)), ((), ())), preferred_element_type=jnp.float32
    )


def on_device(
    spectrum,
    mask,
    courant,
    proj_a,
    proj_b,
    proj_c,
    proj_d,
    stokes_kernel,
    tile_points,
    tile_counts,
    tile_nbr,
    vorticity,
    diffusivity,
):
    comps, rows, lon = spectrum.shape
    margin = 2 * ADV
    bands, dests = lax.axis_size("lat"), lax.axis_size("comp")
    band_index = lax.axis_index("lat")
    sea = jnp.pad(mask.astype(jnp.float32), ((margin, margin), (0, 0)))
    mask_rows = lax.dynamic_slice_in_dim(sea, band_index * rows, rows + 2 * margin, 0)
    up = [(i, i + 1) for i in range(bands - 1)]
    down = [(j, i) for i, j in up]

    def edge(part):
        return lax.optimization_barrier(part).astype(jnp.bfloat16).transpose(1, 0, 2)

    halo_up = lax.ppermute(edge(spectrum[:, rows - margin :]), "lat", up)
    halo_dn = lax.ppermute(edge(spectrum[:, :margin]), "lat", down)
    weights = [lax.all_gather(w, "comp", axis=0, tiled=True) for w in (proj_a, proj_b, proj_c, proj_d)]
    bands_of, points_of = [], []
    width = pl.cdiv(pl.cdiv(comps, CB), PIECES) * CB
    for first in range(0, comps, width):
        piece = advect(
            spectrum, halo_up, halo_dn, mask_rows, courant.T, dests, first, min(width, comps - first)
        )
        bands_of.append(piece)
        points_of.append(lax.all_to_all(piece.astype(jnp.float16), "comp", split_axis=0, concat_axis=0))
    band = jnp.concatenate(bands_of, axis=1)
    points = jnp.concatenate(points_of, axis=1)
    chunk = points.shape[2]
    points = points.reshape(dests * comps, chunk)
    own = points.astype(jnp.float32)
    points = own.astype(jnp.bfloat16)
    product = (contract(weights[0], points) * contract(weights[1], points)).astype(jnp.bfloat16)
    delta = time_step * (contract(weights[2], product) - own * contract(weights[3], product))
    profile = lax.dot_general(
        stokes_kernel, own + delta, (((0,), (0,)), ((), ())), precision=lax.Precision.HIGHEST
    ).astype(jnp.bfloat16)
    group = lax.all_gather(profile, "comp", axis=1, tiled=True)
    back = lax.all_to_all(
        delta.astype(jnp.bfloat16).reshape(dests, comps, chunk), "comp", split_axis=0, concat_axis=0
    )
    force = ocean(group, tile_points[0, 0], tile_counts[0, 0], tile_nbr[0, 0], vorticity[0, 0], diffusivity[0, 0])
    return finish(band, back, rows, lon), force[None, None]


def solution(mesh):
    return jax.shard_map(
        on_device,
        mesh=mesh,
        in_specs=(
            P("comp", "lat", None),
            P(),
            P(None, "comp"),
            P("comp", None),
            P("comp", None),
            P("comp", None),
            P("comp", None),
            P(),
            P("lat", "comp", None),
            P("lat", "comp"),
            P("lat", "comp", None, None),
            P("lat", "comp", None, None),
            P("lat", "comp", None, None),
        ),
        out_specs=(P("comp", "lat", None), P("lat", "comp", None, None)),
        check_vma=False,
    )
```
